32 devices in a mesh: seq: 8 (over z, y), head: 4 (over x, core).
Axes of the slice: x: 2, y: 2, z: 4, core: 2. Of those that a mesh axis runs over, the one named last changes fastest.
Arguments:
- query: bfloat16 [4096, 8192], P('seq', 'head'), may hold values from -1.5 to 1.5
- key_in: bfloat16 [4096, 8192], P('seq', 'head'), may hold values from -0.5 to 0.5
- value: bfloat16 [4096, 8192], P('seq', 'head'), may hold values from -6 to 6
- gate: bfloat16 [4096, 8192], P(('seq', 'head')), may hold values from -6 to 6
- gain: float32 [8192], replicated, may hold values from 0.5 to 1.5
- grad_out: bfloat16 [4096, 8192], P(('seq', 'head')), may hold values from -6 to 6
Outputs:
- grad_query: bfloat16 [4096, 8192], P('seq', 'head')
- grad_key: bfloat16 [4096, 8192], P('seq', 'head')
- grad_value: bfloat16 [4096, 8192], P('seq', 'head')
- grad_gate: bfloat16 [4096, 8192], P(('seq', 'head'))
The draws below stay inside these ranges and needn't reach their ends.
All inputs are finite; a program needn't handle non-finite values.
Results may differ from the reference program's by a relative error of at most 0.012.
Values may be sent and summed in bfloat16 or wider, within the bound.
A program may use at most 128 MiB of HBM per device.

```python
import jax
import jax.numpy as jnp
from jax import lax

HEADS = 64
HEAD_DIM = 128
TOK_DEV = 512
TOKENS = 4096
WIDTH = 8192
N_SEQ = 8


def block_scale(key, dims, shards, least, high):
    level = 1.0
    for dim, shards_of in shards:
        heights = jax.random.uniform(jax.random.fold_in(jax.random.fold_in(key, 6), dim), (shards_of,), jnp.float32, least / len(shards), high / len(shards))
        level = level * jnp.repeat(jnp.exp(heights), dims[dim] // shards_of).reshape((-1,) + (1,) * (len(dims) - 1 - dim))
    return level


def centred(own_key, shape, deviation, most, split=(), kind=jnp.bfloat16):
    level = block_scale(own_key, shape, split, -0.22, 0.18) if split else 1.0
    entries = jax.random.normal(own_key, shape, jnp.float32) * deviation * level
    return jnp.minimum(jnp.maximum(entries, -most), most).astype(kind)


def setup_inputs(seed: int = 0) -> dict:
    seeds = jax.random.split(jax.random.key(seed), 7)
    return {
        "query": centred(seeds[0], (TOKENS, WIDTH), 0.25, 1.5, ((0, 8), (1, 4))),
        "key_in": centred(seeds[1], (TOKENS, WIDTH), HEAD_DIM ** -0.5, 0.5, ((0, 8), (1, 4))),
        "value": centred(seeds[2], (TOKENS, WIDTH), 1.0, 6.0, ((0, 8), (1, 4))),
        "gate": centred(seeds[3], (TOKENS, WIDTH), 1.0, 6.0, ((0, 32),)),
        "gain": jnp.clip(1.0 + 0.1 * jax.random.normal(seeds[4], (WIDTH,), jnp.float32), 0.5, 1.5),
        "grad_out": centred(seeds[5], (TOKENS, WIDTH), 1.0, 6.0, ((0, 32),)),
    }


def reference(query, key_in, value, gate, gain, grad_out):
    blocks = N_SEQ
    tok_block = TOK_DEV
    width_all = HEADS * HEAD_DIM
    queries = query.reshape(blocks, tok_block, HEADS, HEAD_DIM)
    keys_all = key_in.reshape(blocks, tok_block, HEADS, HEAD_DIM)
    values_all = value.reshape(blocks, tok_block, HEADS, HEAD_DIM)
    block_state = jnp.einsum('bthd,bthe->bhde', keys_all.astype(jnp.float32), values_all.astype(jnp.float32))
    zero_state = jnp.zeros((1, HEADS, HEAD_DIM, HEAD_DIM), jnp.float32)
    prefix = jnp.concatenate([zero_state, jnp.cumsum(block_state[:-1], axis=0)], axis=0)
    causal = jnp.tril(jnp.ones((tok_block, tok_block), dtype=bool))

    def forward_block(operands):
        q_block, k_block, v_block, p_block = operands
        scores = jnp.einsum('thd,shd->hts', q_block.astype(jnp.float32), k_block.astype(jnp.float32))
        masked_scores = jnp.where(causal[None], scores, 0.0).astype(jnp.bfloat16)
        prefix_low = p_block.astype(jnp.bfloat16)
        result = jnp.einsum('hts,she->the', masked_scores.astype(jnp.float32), v_block.astype(jnp.float32))
        result = result + jnp.einsum('thd,hde->the', q_block.astype(jnp.float32), prefix_low.astype(jnp.float32))
        return result.astype(jnp.bfloat16)
    attn_out = lax.map(forward_block, (queries, keys_all, values_all, prefix))
    attn_out = attn_out.reshape(blocks, tok_block, width_all)
    gate_blocks = gate.reshape(blocks, tok_block, width_all)
    grad_blocks = grad_out.reshape(blocks, tok_block, width_all)

    def norm_block(operands):
        out_block, gate_block, grad_block = operands
        rows_wide = out_block.astype(jnp.float32)
        inv_rms = lax.rsqrt(lax.optimization_barrier(jnp.mean(rows_wide * rows_wide, axis=1, keepdims=True)) + 1e-06)
        normed = rows_wide * inv_rms
        gate_wide = gate_block.astype(jnp.float32)
        sigmoid_gate = jax.nn.sigmoid(gate_wide)
        scaled = grad_block.astype(jnp.float32) * gain[None, :]
        grad_gate = (scaled * normed * sigmoid_gate * (1.0 + gate_wide * (1.0 - sigmoid_gate))).astype(jnp.bfloat16)
        weighted = scaled * gate_wide * sigmoid_gate
        grad_attn = inv_rms * (weighted - normed * lax.optimization_barrier(jnp.mean(weighted * normed, axis=1, keepdims=True)))
        return (grad_attn.astype(jnp.bfloat16), grad_gate)
    grad_attn, grad_gate = lax.map(norm_block, (attn_out, gate_blocks, grad_blocks))
    grad_attn = grad_attn.reshape(blocks, tok_block, HEADS, HEAD_DIM)
    block_grad = jnp.einsum('bthd,bthe->bhde', queries.astype(jnp.float32), grad_attn.astype(jnp.float32))
    flipped = jnp.flip(block_grad, axis=0)
    suffix = jnp.flip(jnp.concatenate([zero_state, jnp.cumsum(flipped[:-1], axis=0)], axis=0), axis=0)

    def backward_block(operands):
        q_block, k_block, v_block, do_block, p_block, s_block = operands
        q_wide = q_block.astype(jnp.float32)
        k_wide = k_block.astype(jnp.float32)
        v_wide = v_block.astype(jnp.float32)
        do_wide = do_block.astype(jnp.float32)
        prefix_low = p_block.astype(jnp.bfloat16).astype(jnp.float32)
        suffix_low = s_block.astype(jnp.bfloat16).astype(jnp.float32)
        scores = jnp.einsum('thd,shd->hts', q_wide, k_wide)
        masked_scores = jnp.where(causal[None], scores, 0.0).astype(jnp.bfloat16).astype(jnp.float32)
        grad_scores = jnp.where(causal[None], jnp.einsum('the,she->hts', do_wide, v_wide), 0.0)
        grad_scores = grad_scores.astype(jnp.bfloat16).astype(jnp.float32)
        grad_query = jnp.einsum('hts,shd->thd', grad_scores, k_wide) + jnp.einsum('the,hde->thd', do_wide, prefix_low)
        grad_key = jnp.einsum('hts,thd->shd', grad_scores, q_wide) + jnp.einsum('she,hde->shd', v_wide, suffix_low)
        grad_value = jnp.einsum('hts,the->she', masked_scores, do_wide) + jnp.einsum('shd,hde->she', k_wide, suffix_low)
        return (grad_query.astype(jnp.bfloat16), grad_key.astype(jnp.bfloat16), grad_value.astype(jnp.bfloat16))
    grad_query, grad_key, grad_value = lax.map(backward_block, (queries, keys_all, values_all, grad_attn, prefix, suffix))
    total_rows = blocks * tok_block
    return (grad_query.reshape(total_rows, width_all), grad_key.reshape(total_rows, width_all), grad_value.reshape(total_rows, width_all), grad_gate.reshape(total_rows, width_all))
```

```python
import functools

import jax
import jax.numpy as jnp
from jax import lax
from jax.experimental import pallas as pl
from jax.experimental.pallas import tpu as pltpu
from jax.sharding import PartitionSpec as P

HEAD_DIM = 128
EPS = 1e-06
MESH = pl.DeviceIdType.MESH
F32 = jnp.float32
BF16 = jnp.bfloat16
CHUNKS = 4
GROUP = 4


def dot_nn(a, b):
    return lax.dot_general(a, b, (((1,), (0,)), ((), ())), preferred_element_type=F32)


def dot_nt(a, b):
    return lax.dot_general(a, b, (((1,), (1,)), ((), ())), preferred_element_type=F32)


def dot_tn(a, b):
    return lax.dot_general(a, b, (((0,), (0,)), ((), ())), preferred_element_type=F32)


def body(
    n_seq, n_head,
    q_h, k_h, v_h, gate_h, gain_h, go_h,
    gqv, ggv, acc_a, acc_b, suf, k, v,
    q, gate, gain, go,
    wsend, wbuf, g2, attn, d_o, arows,
    st, st_p, st_c, st_o, st_r, pre,
    gst, gst_p, gst_c, gst_o, gst_r,
    scores, squares, crossed, stat_s, stat_r, inv_b, c_b,
    in_sem, part_sem,
    w_ss, w_rs, a_ss, a_rs, s_ss, s_rs,
    m_ss, m_rs, c_ss, c_rs, r_ss, r_rs,
    gm_ss, gm_rs, gc_ss, gc_rs, gr_ss, gr_rs,
):
    hd = HEAD_DIM
    tok, cols = q.shape
    rows, width = gate.shape
    heads = cols // hd
    half = tok // 2
    mine = heads // 2
    n_pair = mine // 2
    chunk = cols // CHUNKS
    idx = lax.axis_index("seq")
    me = lax.axis_index("head")
    side = lax.rem(idx, 2)
    partner = idx + 1 - 2 * side
    has_below = idx >= 2
    has_above = idx + 2 < n_seq
    n_x = n_head // 2
    at_x = me // 2
    core = lax.rem(me, 2)
    peers = [(dx, dc) for dx in range(1, n_x) for dc in range(2)] + [(0, 1)]
    crossing = list(range(len(peers) - 1))
    beside = len(peers) - 1
    own_head = side * mine
    mate_head = (1 - side) * mine

    def to_peer(p):
        dx, dc = peers[p]
        return lax.rem(at_x + dx, n_x) * 2 + lax.rem(core + dc, 2)

    def from_peer(p):
        dx, dc = peers[p]
        return lax.rem(at_x + n_x - dx, n_x) * 2 + lax.rem(core + dc, 2)

    def row_block(shard):
        return pl.ds(pl.multiple_of(shard * rows, rows), rows)

    def col_block(shard):
        return pl.ds(pl.multiple_of(shard * cols, cols), cols)

    def col_chunk(shard, c):
        return pl.ds(pl.multiple_of(shard * cols + c * chunk, chunk), chunk)

    def head_cols(h):
        return pl.ds(pl.multiple_of(h * hd, hd), hd)

    whole_loads = [
        pltpu.make_async_copy(src, dst, in_sem.at[i])
        for i, (src, dst) in enumerate(((gain_h, gain), (k_h, k), (v_h, v), (q_h, q)))
    ]

    def part_load(i, shard):
        at = col_block(shard)
        return [
            pltpu.make_async_copy(gate_h.at[:, at], gate.at[:, at], part_sem.at[2 * i]),
            pltpu.make_async_copy(go_h.at[:, at], go.at[:, at], part_sem.at[2 * i + 1]),
        ]

    shards = [to_peer(p) for p in range(len(peers))] + [me]
    part_loads = [part_load(i, shard) for i, shard in enumerate(shards)]
    whole_loads[0].start()
    for load in part_loads[0]:
        load.start()
    whole_loads[1].start()
    whole_loads[2].start()
    for part in part_loads[1:]:
        for load in part:
            load.start()
    whole_loads[3].start()

    barrier = pltpu.get_barrier_semaphore()
    for p in range(len(peers)):
        pl.semaphore_signal(barrier, inc=1, device_id={"head": to_peer(p)}, device_id_type=MESH)
    pl.semaphore_signal(barrier, inc=1, device_id={"seq": partner}, device_id_type=MESH)

    @pl.when(has_below)
    def _():
        pl.semaphore_signal(barrier, inc=1, device_id={"seq": idx - 2}, device_id_type=MESH)

    @pl.when(has_above)
    def _():
        pl.semaphore_signal(barrier, inc=1, device_id={"seq": idx + 2}, device_id_type=MESH)

    bc = 256

    def weigh(shard, local):
        def step(i, carry):
            c = pl.multiple_of(i * bc, bc)
            at = pl.ds(pl.multiple_of(shard * cols + c, bc), bc)
            g = gate[:, at].astype(F32)
            scaled = go[:, at].astype(F32) * gain[:, at]
            sig = jax.nn.sigmoid(g)
            part = scaled * sig
            g2[:, at] = part * (1.0 + g * (1.0 - sig))
            weighted = (part * g).astype(BF16)
            if local:
                wbuf[row_block(me), pl.ds(c, bc)] = weighted
            else:
                wsend[:, at] = weighted
            return carry

        lax.fori_loop(0, cols // bc, step, 0)

    def w_copy(p, c):
        to, i = to_peer(p), p * CHUNKS + c
        return pltpu.make_async_remote_copy(
            src_ref=wsend.at[:, col_chunk(to, c)],
            dst_ref=wbuf.at[row_block(me), col_chunk(0, c)],
            send_sem=w_ss.at[i], recv_sem=w_rs.at[i],
            device_id={"head": to}, device_id_type=MESH,
        )

    def w_arrival(p, c):
        to, i = to_peer(p), p * CHUNKS + c
        return pltpu.make_async_remote_copy(
            src_ref=wsend.at[:, col_chunk(to, c)],
            dst_ref=wbuf.at[row_block(from_peer(p)), col_chunk(0, c)],
            send_sem=w_ss.at[i], recv_sem=w_rs.at[i],
            device_id={"head": to}, device_id_type=MESH,
        )

    def a_copy(p, c):
        to, i = to_peer(p), p * CHUNKS + c
        return pltpu.make_async_remote_copy(
            src_ref=attn.at[row_block(to), col_chunk(0, c)],
            dst_ref=arows.at[:, col_chunk(me, c)],
            send_sem=a_ss.at[i], recv_sem=a_rs.at[i],
            device_id={"head": to}, device_id_type=MESH,
        )

    def a_arrival(p, c):
        to, i = to_peer(p), p * CHUNKS + c
        return pltpu.make_async_remote_copy(
            src_ref=attn.at[row_block(to), col_chunk(0, c)],
            dst_ref=arows.at[:, col_chunk(from_peer(p), c)],
            send_sem=a_ss.at[i], recv_sem=a_rs.at[i],
            device_id={"head": to}, device_id_type=MESH,
        )

    def s_copy(p):
        return pltpu.make_async_remote_copy(
            src_ref=stat_s, dst_ref=stat_r.at[p],
            send_sem=s_ss.at[p], recv_sem=s_rs.at[p],
            device_id={"head": to_peer(p)}, device_id_type=MESH,
        )

    def pair_copy(src, dst, ss, rs, base, j, target):
        at = pl.ds(base + 2 * j, 2)
        return pltpu.make_async_remote_copy(
            src_ref=src.at[at], dst_ref=dst.at[at],
            send_sem=ss.at[j], recv_sem=rs.at[j],
            device_id={"seq": target}, device_id_type=MESH,
        )

    def weigh_and_send(p):
        weigh(to_peer(p), False)
        if p == 0:
            below, above = has_below.astype(jnp.int32), has_above.astype(jnp.int32)
            pl.semaphore_wait(barrier, n_head + below + above)
        for c in range(CHUNKS):
            w_copy(p, c).start()

    def wait_part(i):
        for load in part_loads[i]:
            load.wait()

    whole_loads[0].wait()
    wait_part(0)
    weigh_and_send(0)
    whole_loads[1].wait()
    whole_loads[2].wait()

    def states(base, send):
        def step(i, carry):
            first = base + GROUP * i
            for t in range(GROUP):
                sl = head_cols(first + t)
                st[first + t] = dot_tn(k[:, sl], v[:, sl]).astype(BF16)
            if send:
                for t in range(GROUP // 2):
                    pair_copy(st, st_p, m_ss, m_rs, base, i * (GROUP // 2) + t, partner).start()
            return carry

        lax.fori_loop(0, mine // GROUP, step, 0)

    states(mate_head, True)
    for p in range(1, len(peers)):
        wait_part(p)
        weigh_and_send(p)
    states(own_head, False)
    wait_part(len(peers))
    weigh(me, True)
    whole_loads[3].wait()

    def pass_on(j, own, mate, chain, out, given, kept, sems, source_ok, target_ok, target, wants):
        mate_ss, mate_rs, chain_ss, chain_rs, give_ss, give_rs = sems
        at = pl.ds(own_head + 2 * j, 2)
        pair_copy(own, mate, mate_ss, mate_rs, own_head, j, partner).wait_recv()

        @pl.when(source_ok)
        def _():
            pair_copy(out, chain, chain_ss, chain_rs, own_head, j, target).wait_recv()

        @pl.when(jnp.logical_not(source_ok))
        def _():
            chain[at] = jnp.zeros((2, hd, hd), BF16)

        @pl.when(target_ok)
        def _():
            out[at] = (
                chain[at].astype(F32) + mate[at].astype(F32) + own[at].astype(F32)
            ).astype(BF16)
            pair_copy(out, chain, chain_ss, chain_rs, own_head, j, target).start()

        before = chain[at].astype(F32)
        weight = wants.astype(F32)
        given[at] = (before + (1.0 - weight) * own[at].astype(F32)).astype(BF16)
        pair_copy(given, kept, give_ss, give_rs, own_head, j, partner).start()
        kept[at] = (before + weight * mate[at].astype(F32)).astype(BF16)

    at_row = lax.broadcasted_iota(jnp.int32, (half, half), 0)
    at_col = lax.broadcasted_iota(jnp.int32, (half, half), 1)

    def lower(x):
        return jnp.where(at_row >= at_col, x, 0.0).astype(BF16)

    def upper(x):
        return jnp.where(at_row <= at_col, x, 0.0).astype(BF16)

    depth = idx // 2
    length = n_seq // 2

    def forward_local(h):
        sl = head_cols(h)
        q0, q1 = q[:half, sl], q[half:, sl]
        k0, k1 = k[:half, sl], k[half:, sl]
        v0, v1 = v[:half, sl], v[half:, sl]
        acc_a[:half, sl] = dot_nn(lower(dot_nt(q0, k0)), v0)
        acc_a[half:, sl] = dot_nn(dot_nt(q1, k0).astype(BF16), v0) + dot_nn(
            lower(dot_nt(q1, k1)), v1
        )
        scores[h, 0] = upper(dot_nt(k0, q0))
        scores[h, 1] = dot_nt(k0, q1).astype(BF16)
        scores[h, 2] = upper(dot_nt(k1, q1))

    def attend(first):
        for t in range(2):
            sl = head_cols(first + t)
            attn[:, sl] = (acc_a[:, sl] + dot_nn(q[:, sl], pre[first + t])).astype(BF16)

    late = jnp.maximum(depth + 2, n_pair)

    def forward(i, carry):
        @pl.when(i < 2 * n_pair)
        def _():
            for t in range(2):
                forward_local(lax.rem(own_head + 2 * i + t, heads))

        j = i - depth

        @pl.when((j >= 0) & (j < n_pair))
        def _():
            pass_on(
                j, st, st_p, st_c, st_o, st_r, pre,
                (m_ss, m_rs, c_ss, c_rs, r_ss, r_rs),
                has_below, has_above, idx + 2, side,
            )
            attend(own_head + 2 * j)

        m = i - late

        @pl.when((m >= 0) & (m < n_pair))
        def _():
            pair_copy(st_r, pre, r_ss, r_rs, mate_head, m, partner).wait_recv()
            attend(mate_head + 2 * m)

        return carry

    lax.fori_loop(0, max(length + 1 + n_pair, 2 * n_pair), forward, 0)

    br = 128

    def sums(c, carry):
        for p in range(len(peers)):
            w_arrival(p, c).wait_recv()

        def step(i, inner):
            rs = pl.ds(pl.multiple_of(i * br, br), br)
            s0 = jnp.zeros((br, hd), F32)
            s1 = jnp.zeros((br, hd), F32)
            for u in range(chunk // hd):
                at = pl.ds(pl.multiple_of(c * chunk + u * hd, hd), hd)
                a = attn[rs, at].astype(F32)
                w = wbuf[rs, at].astype(F32)
                s0 = s0 + a * a
                s1 = s1 + a * w
            squares[rs, :] += s0
            crossed[rs, :] += s1
            return inner

        lax.fori_loop(0, tok // br, step, 0)
        return carry

    squares[...] = jnp.zeros_like(squares)
    crossed[...] = jnp.zeros_like(crossed)
    lax.fori_loop(0, CHUNKS, sums, 0)
    n_row = tok // hd
    s0 = jnp.sum(jnp.transpose(squares[...]), axis=0, keepdims=True)
    s1 = jnp.sum(jnp.transpose(crossed[...]), axis=0, keepdims=True)
    for r in range(n_row):
        stat_s[r:r + 1, :] = s0[:, r * hd:(r + 1) * hd]
        stat_s[n_row + r:n_row + r + 1, :] = s1[:, r * hd:(r + 1) * hd]
    for p in range(len(peers)):
        s_copy(p).start()
    for c in range(CHUNKS):
        for p in range(len(peers)):
            a_copy(p, c).start()
    total = stat_s[...]
    for p in range(len(peers)):
        s_copy(p).wait_recv()
    for p in range(len(peers)):
        total = total + stat_r[p]
    inv = lax.rsqrt(total[:n_row] / width + EPS)
    c_all = inv * inv * (total[n_row:2 * n_row] / width)
    for r in range(n_row):
        inv_b[r * hd:(r + 1) * hd, :] = jnp.transpose(
            jnp.broadcast_to(inv[r:r + 1], (hd, hd))
        )
        c_b[r * hd:(r + 1) * hd, :] = jnp.transpose(
            jnp.broadcast_to(c_all[r:r + 1], (hd, hd))
        )

    def grads(base, send):
        def step(i, carry):
            first = base + GROUP * i
            for t in range(GROUP):
                sl = head_cols(first + t)
                a = attn[:, sl].astype(F32)
                grad = (inv_b[...] * (wbuf[:, sl].astype(F32) - a * c_b[...])).astype(BF16)
                d_o[:, sl] = grad
                gst[first + t] = dot_tn(q[:, sl], grad).astype(BF16)
            if send:
                for t in range(GROUP // 2):
                    pair_copy(gst, gst_p, gm_ss, gm_rs, base, i * (GROUP // 2) + t, partner).start()
            return carry

        lax.fori_loop(0, mine // GROUP, step, 0)

    grads(mate_head, True)
    grads(own_head, False)

    def backward_local(h):
        sl = head_cols(h)
        q0, q1 = q[:half, sl], q[half:, sl]
        k0, k1 = k[:half, sl], k[half:, sl]
        v0, v1 = v[:half, sl], v[half:, sl]
        d0, d1 = d_o[:half, sl], d_o[half:, sl]
        before = pre[h]
        gqv[:half, sl] = (dot_nn(lower(dot_nt(d0, v0)), k0) + dot_nt(d0, before)).astype(BF16)
        gqv[half:, sl] = (
            dot_nn(dot_nt(d1, v0).astype(BF16), k0)
            + dot_nn(lower(dot_nt(d1, v1)), k1)
            + dot_nt(d1, before)
        ).astype(BF16)
        acc_a[:half, sl] = dot_nn(upper(dot_nt(v0, d0)), q0) + dot_nn(
            dot_nt(v0, d1).astype(BF16), q1
        )
        acc_a[half:, sl] = dot_nn(upper(dot_nt(v1, d1)), q1)
        acc_b[:half, sl] = dot_nn(scores[h, 0], d0) + dot_nn(scores[h, 1], d1)
        acc_b[half:, sl] = dot_nn(scores[h, 2], d1)

    above_me = length - 1 - depth
    back_lag = (3 * above_me + 1) // 2

    def backward(i, carry):
        @pl.when(i < 2 * n_pair)
        def _():
            for t in range(2):
                backward_local(2 * i + t)

        j = i - back_lag

        @pl.when((j >= 0) & (j < n_pair))
        def _():
            pass_on(
                j, gst, gst_p, gst_c, gst_o, gst_r, suf,
                (gm_ss, gm_rs, gc_ss, gc_rs, gr_ss, gr_rs),
                has_above, has_below, idx - 2, 1 - side,
            )

        return carry

    lax.fori_loop(0, max(2 * n_pair, (3 * (length - 1) + 1) // 2 + n_pair), backward, 0)

    def finish(shard, c, local):
        scale = inv_b[row_block(me), :]
        for u in range(chunk // hd):
            at = pl.ds(pl.multiple_of(shard * cols + c * chunk + u * hd, hd), hd)
            if local:
                here = pl.ds(pl.multiple_of(c * chunk + u * hd, hd), hd)
                a = attn[row_block(me), here]
            else:
                a = arows[:, at]
            ggv[:, at] = (g2[:, at] * (a.astype(F32) * scale)).astype(BF16)

    def finish_local(c, carry):
        finish(me, c, True)
        return carry

    lax.fori_loop(0, CHUNKS, finish_local, 0)

    def finish_beside(c, carry):
        a_arrival(beside, c).wait_recv()
        finish(from_peer(beside), c, False)
        return carry

    lax.fori_loop(0, CHUNKS, finish_beside, 0)

    def drain(j, carry):
        pair_copy(st, st_p, m_ss, m_rs, mate_head, j, partner).wait_send()
        pair_copy(st_r, pre, r_ss, r_rs, own_head, j, partner).wait_send()
        pair_copy(gst, gst_p, gm_ss, gm_rs, mate_head, j, partner).wait_send()
        pair_copy(gst_r, suf, gr_ss, gr_rs, own_head, j, partner).wait_send()
        pair_copy(gst_r, suf, gr_ss, gr_rs, mate_head, j, partner).wait_recv()

        @pl.when(has_above)
        def _():
            pair_copy(st_o, st_c, c_ss, c_rs, own_head, j, idx + 2).wait_send()

        @pl.when(has_below)
        def _():
            pair_copy(gst_o, gst_c, gc_ss, gc_rs, own_head, j, idx - 2).wait_send()

        return carry

    lax.fori_loop(0, n_pair, drain, 0)
    for p in range(len(peers)):
        s_copy(p).wait_send()
        for c in range(CHUNKS):
            w_copy(p, c).wait_send()

    def finish_crossing(c, carry):
        for p in crossing:
            a_arrival(p, c).wait_recv()
            finish(from_peer(p), c, False)
        return carry

    lax.fori_loop(0, CHUNKS, finish_crossing, 0)
    for p in range(len(peers)):
        for c in range(CHUNKS):
            a_copy(p, c).wait_send()


def store(gq, gg, acc_a, acc_b, suf, k, v, gq_h, gk_h, gv_h, gg_h, gk, gv, sem, k_sem, v_sem):
    hd = HEAD_DIM
    tok, cols = gq.shape
    span = GROUP * hd
    ready = [
        pltpu.make_async_copy(src, dst, sem.at[i])
        for i, (src, dst) in enumerate(((gq, gq_h), (gg, gg_h)))
    ]
    for copy in ready:
        copy.start()

    def copies(i):
        at = pl.ds(pl.multiple_of(i * span, span), span)
        return (
            pltpu.make_async_copy(gk.at[:, at], gk_h.at[:, at], k_sem.at[i]),
            pltpu.make_async_copy(gv.at[:, at], gv_h.at[:, at], v_sem.at[i]),
        )

    def add_later(i, carry):
        for t in range(GROUP):
            h = GROUP * i + t
            sl = pl.ds(pl.multiple_of(h * hd, hd), hd)
            after = suf[h]
            gk[:, sl] = (acc_a[:, sl] + dot_nt(v[:, sl], after)).astype(BF16)
            gv[:, sl] = (acc_b[:, sl] + dot_nn(k[:, sl], after)).astype(BF16)
        for copy in copies(i):
            copy.start()
        return carry

    groups = cols // span
    lax.fori_loop(0, groups, add_later, 0)
    for copy in ready:
        copy.wait()
    for i in range(groups):
        for copy in copies(i):
            copy.wait()


def on_device(n_seq, n_head, query, key_in, value, gate, gain, grad_out):
    tok, cols = query.shape
    rows, width = gate.shape
    heads = cols // HEAD_DIM
    groups = heads // GROUP
    wide = pltpu.VMEM((tok, cols), BF16)
    thin = pltpu.VMEM((rows, width), BF16)
    state = pltpu.VMEM((heads, HEAD_DIM, HEAD_DIM), BF16)
    token = pltpu.VMEM((tok, HEAD_DIM), F32)
    sum_of = pltpu.VMEM((tok, cols), F32)
    tile = (2 * tok // HEAD_DIM, HEAD_DIM)
    by_part = pltpu.SemaphoreType.DMA(((n_head - 1) * CHUNKS,))
    by_peer = pltpu.SemaphoreType.DMA((n_head - 1,))
    by_pair = pltpu.SemaphoreType.DMA((heads // 4,))
    anywhere = pl.BlockSpec(memory_space=pl.ANY)
    on_chip = pl.BlockSpec(memory_space=pltpu.VMEM)
    results = pl.pallas_call(
        functools.partial(body, n_seq, n_head),
        out_shape=[wide, thin, sum_of, sum_of, state, wide, wide],
        in_specs=[anywhere] * 6,
        out_specs=[on_chip] * 7,
        scratch_shapes=[
            wide, thin, pltpu.VMEM((1, width), F32), thin,
            thin, wide, pltpu.VMEM((rows, width), F32), wide, wide, thin,
            state, state, state, state, state, state,
            state, state, state, state, state,
            pltpu.VMEM((heads, 3, tok // 2, tok // 2), BF16),
            token, token, pltpu.VMEM(tile, F32), pltpu.VMEM((n_head - 1, *tile), F32), token, token,
            pltpu.SemaphoreType.DMA((4,)), pltpu.SemaphoreType.DMA((2 * n_head,)),
            by_part, by_part, by_part, by_part, by_peer, by_peer,
            by_pair, by_pair, by_pair, by_pair, by_pair, by_pair,
            by_pair, by_pair, by_pair, by_pair, by_pair, by_pair,
        ],
        compiler_params=pltpu.CompilerParams(
            collective_id=0, has_side_effects=True, vmem_limit_bytes=44 * 2**20
        ),
        name="linear_attention_backward",
    )(query, key_in, value, gate, gain.reshape(1, width), grad_out)
    wide_out = jax.ShapeDtypeStruct((tok, cols), BF16)
    return pl.pallas_call(
        store,
        out_shape=[wide_out, wide_out, wide_out, jax.ShapeDtypeStruct((rows, width), BF16)],
        in_specs=[on_chip] * 7,
        out_specs=[anywhere] * 4,
        scratch_shapes=[
            wide, wide, pltpu.SemaphoreType.DMA((2,)),
            pltpu.SemaphoreType.DMA((groups,)), pltpu.SemaphoreType.DMA((groups,)),
        ],
        compiler_params=pltpu.CompilerParams(vmem_limit_bytes=6 * 2**20),
        name="store_gradients",
    )(*[pltpu.with_memory_space_constraint(x, pltpu.VMEM) for x in results])


def solution(mesh):
    in_specs = (
        P("seq", "head"),
        P("seq", "head"),
        P("seq", "head"),
        P(("seq", "head"), None),
        P(),
        P(("seq", "head"), None),
    )
    out_specs = (P("seq", "head"), P("seq", "head"), P("seq", "head"), P(("seq", "head"), None))
    return jax.shard_map(
        functools.partial(on_device, mesh.shape["seq"], mesh.shape["head"]),
        mesh=mesh, in_specs=in_specs, out_specs=out_specs, check_vma=False,
    )
```

```python
import functools

import jax
import jax.numpy as jnp
from jax import lax
from jax.experimental import pallas as pl
from jax.experimental.pallas import tpu as pltpu
from jax.sharding import PartitionSpec as P

HEAD_DIM = 128
EPS = 1e-06
MESH = pl.DeviceIdType.MESH
F32 = jnp.float32
BF16 = jnp.bfloat16
CHUNKS = 4
GROUP = 4
FORWARD_LAG = 3
BACKWARD_LAG = 3
GIVE_LAG = 3


def dot_nn(a, b):
    return lax.dot_general(a, b, (((1,), (0,)), ((), ())), preferred_element_type=F32)


def dot_nt(a, b):
    return lax.dot_general(a, b, (((1,), (1,)), ((), ())), preferred_element_type=F32)


def dot_tn(a, b):
    return lax.dot_general(a, b, (((0,), (0,)), ((), ())), preferred_element_type=F32)


def body(
    n_seq, n_head,
    q_h, k_h, v_h, gate_h, gain_h, go_h,
    gqv, ggv, acc_a, acc_b, suf, k, v,
    q, gate, gain, go,
    wsend, wbuf, g2, attn, d_o, arows,
    st, st_p, st_c, st_o, st_r, pre,
    gst, gst_p, gst_c, gst_o, gst_r,
    scores, low_a, up_a, low_b, up_b, squares, crossed, stat_s, stat_r, inv_b, c_b,
    in_sem, part_sem, first_sem,
    w_ss, w_rs, a_ss, a_rs, s_ss, s_rs,
    m_ss, m_rs, c_ss, c_rs, r_ss, r_rs,
    gm_ss, gc_ss, gr_ss,
):
    hd = HEAD_DIM
    tok, cols = q.shape
    rows, width = gate.shape
    heads = cols // hd
    half = tok // 2
    mine = heads // 2
    chunk = cols // CHUNKS
    idx = lax.axis_index("seq")
    me = lax.axis_index("head")
    side = lax.rem(idx, 2)
    partner = idx + 1 - 2 * side
    has_below = idx >= 2
    has_above = idx + 2 < n_seq
    n_x = n_head // 2
    at_x = me // 2
    core = lax.rem(me, 2)
    peers = [(dx, dc) for dx in range(1, n_x) for dc in range(2)] + [(0, 1)]
    crossing = list(range(len(peers) - 1))
    beside = len(peers) - 1
    own_head = side * mine
    mate_head = (1 - side) * mine

    def to_peer(p):
        dx, dc = peers[p]
        return lax.rem(at_x + dx, n_x) * 2 + lax.rem(core + dc, 2)

    def from_peer(p):
        dx, dc = peers[p]
        return lax.rem(at_x + n_x - dx, n_x) * 2 + lax.rem(core + dc, 2)

    def row_block(shard):
        return pl.ds(pl.multiple_of(shard * rows, rows), rows)

    def col_block(shard):
        return pl.ds(pl.multiple_of(shard * cols, cols), cols)

    def col_chunk(shard, c):
        return pl.ds(pl.multiple_of(shard * cols + c * chunk, chunk), chunk)

    def head_cols(h):
        return pl.ds(pl.multiple_of(h * hd, hd), hd)

    whole_loads = [
        pltpu.make_async_copy(src, dst, in_sem.at[i])
        for i, (src, dst) in enumerate(((gain_h, gain), (k_h, k), (v_h, v), (q_h, q)))
    ]

    def part_load(i, shard):
        at = col_block(shard)
        return [
            pltpu.make_async_copy(gate_h.at[:, at], gate.at[:, at], part_sem.at[2 * i]),
            pltpu.make_async_copy(go_h.at[:, at], go.at[:, at], part_sem.at[2 * i + 1]),
        ]

    shards = [to_peer(p) for p in range(len(peers))] + [me]
    part_loads = [part_load(i, shard) for i, shard in enumerate(shards)]

    def first_load(c):
        at = col_chunk(shards[0], c)
        return [
            pltpu.make_async_copy(gate_h.at[:, at], gate.at[:, at], first_sem.at[2 * c]),
            pltpu.make_async_copy(go_h.at[:, at], go.at[:, at], first_sem.at[2 * c + 1]),
        ]

    whole_loads[0].start()
    for c in range(CHUNKS):
        for load in first_load(c):
            load.start()
    whole_loads[1].start()
    whole_loads[2].start()
    for part in part_loads[1:]:
        for load in part:
            load.start()
    whole_loads[3].start()

    barrier = pltpu.get_barrier_semaphore()
    for p in range(len(peers)):
        pl.semaphore_signal(barrier, inc=1, device_id={"head": to_peer(p)}, device_id_type=MESH)
    pl.semaphore_signal(barrier, inc=1, device_id={"seq": partner}, device_id_type=MESH)

    @pl.when(has_below)
    def _():
        pl.semaphore_signal(barrier, inc=1, device_id={"seq": idx - 2}, device_id_type=MESH)

    @pl.when(has_above)
    def _():
        pl.semaphore_signal(barrier, inc=1, device_id={"seq": idx + 2}, device_id_type=MESH)

    bc = min(256, chunk)

    def weigh(shard, first, span, local):
        def step(i, carry):
            c = pl.multiple_of(first + i * bc, bc)
            at = pl.ds(pl.multiple_of(shard * cols + c, bc), bc)
            g = gate[:, at].astype(F32)
            scaled = go[:, at].astype(F32) * gain[:, at]
            sig = jax.nn.sigmoid(g)
            part = scaled * sig
            g2[:, at] = part * (1.0 + g * (1.0 - sig))
            weighted = (part * g).astype(BF16)
            if local:
                wbuf[row_block(me), pl.ds(c, bc)] = weighted
            else:
                wsend[:, at] = weighted
            return carry

        lax.fori_loop(0, span // bc, step, 0)

    def w_copy(p, c):
        to, i = to_peer(p), p * CHUNKS + c
        return pltpu.make_async_remote_copy(
            src_ref=wsend.at[:, col_chunk(to, c)],
            dst_ref=wbuf.at[row_block(me), col_chunk(0, c)],
            send_sem=w_ss, recv_sem=w_rs.at[i],
            device_id={"head": to}, device_id_type=MESH,
        )

    def w_arrival(p, c):
        to, i = to_peer(p), p * CHUNKS + c
        return pltpu.make_async_remote_copy(
            src_ref=wsend.at[:, col_chunk(to, c)],
            dst_ref=wbuf.at[row_block(from_peer(p)), col_chunk(0, c)],
            send_sem=w_ss, recv_sem=w_rs.at[i],
            device_id={"head": to}, device_id_type=MESH,
        )

    def a_copy(p, c):
        to, i = to_peer(p), p * CHUNKS + c
        return pltpu.make_async_remote_copy(
            src_ref=attn.at[row_block(to), col_chunk(0, c)],
            dst_ref=arows.at[:, col_chunk(me, c)],
            send_sem=a_ss, recv_sem=a_rs.at[i],
            device_id={"head": to}, device_id_type=MESH,
        )

    def a_arrival(p, c):
        to, i = to_peer(p), p * CHUNKS + c
        return pltpu.make_async_remote_copy(
            src_ref=attn.at[row_block(to), col_chunk(0, c)],
            dst_ref=arows.at[:, col_chunk(from_peer(p), c)],
            send_sem=a_ss, recv_sem=a_rs.at[i],
            device_id={"head": to}, device_id_type=MESH,
        )

    def s_copy(p):
        return pltpu.make_async_remote_copy(
            src_ref=stat_s, dst_ref=stat_r.at[p],
            send_sem=s_ss.at[p], recv_sem=s_rs.at[p],
            device_id={"head": to_peer(p)}, device_id_type=MESH,
        )

    def head_copy(src, dst, ss, rs, base, j, target):
        return pltpu.make_async_remote_copy(
            src_ref=src.at[base + j], dst_ref=dst.at[base + j],
            send_sem=ss, recv_sem=rs.at[j],
            device_id={"seq": target}, device_id_type=MESH,
        )

    def heads_sent(src, dst, ss, rs, base, target):
        at = pl.ds(base, mine)
        pltpu.make_async_remote_copy(
            src_ref=src.at[at], dst_ref=dst.at[at],
            send_sem=ss, recv_sem=rs.at[0],
            device_id={"seq": target}, device_id_type=MESH,
        ).wait_send()

    def weigh_and_send(p):
        weigh(to_peer(p), 0, cols, False)
        for c in range(CHUNKS):
            w_copy(p, c).start()

    def wait_part(i):
        for load in part_loads[i]:
            load.wait()

    whole_loads[0].wait()
    for c in range(CHUNKS):
        for load in first_load(c):
            load.wait()
        weigh(shards[0], c * chunk, chunk, False)
        if c == 0:
            below, above = has_below.astype(jnp.int32), has_above.astype(jnp.int32)
            pl.semaphore_wait(barrier, n_head + below + above)
        w_copy(0, c).start()
    whole_loads[1].wait()
    whole_loads[2].wait()

    def states(base, send):
        def step(i, carry):
            first = base + GROUP * i
            for t in range(GROUP):
                sl = head_cols(first + t)
                st[first + t] = dot_tn(k[:, sl], v[:, sl]).astype(BF16)
            if send:
                for t in range(GROUP):
                    head_copy(st, st_p, m_ss, m_rs, base, i * GROUP + t, partner).start()
            return carry

        lax.fori_loop(0, mine // GROUP, step, 0)

    states(mate_head, True)
    for p in range(1, len(peers)):
        wait_part(p)
        weigh_and_send(p)
    states(own_head, False)
    wait_part(len(peers))
    weigh(me, 0, cols, True)
    whole_loads[3].wait()

    def pass_on(j, own, mate, chain, out, given, kept, sems, source_ok, target_ok, target, wants):
        mate_ss, mate_rs, chain_ss, chain_rs, give_ss, give_rs = sems
        at = own_head + j
        head_copy(own, mate, mate_ss, mate_rs, own_head, j, partner).wait_recv()

        @pl.when(source_ok)
        def _():
            head_copy(out, chain, chain_ss, chain_rs, own_head, j, target).wait_recv()

        @pl.when(jnp.logical_not(source_ok))
        def _():
            chain[at] = jnp.zeros((hd, hd), BF16)

        @pl.when(target_ok)
        def _():
            out[at] = (
                chain[at].astype(F32) + mate[at].astype(F32) + own[at].astype(F32)
            ).astype(BF16)
            head_copy(out, chain, chain_ss, chain_rs, own_head, j, target).start()

        before = chain[at].astype(F32)
        weight = wants.astype(F32)
        given[at] = (before + (1.0 - weight) * own[at].astype(F32)).astype(BF16)
        head_copy(given, kept, give_ss, give_rs, own_head, j, partner).start()
        kept[at] = (before + weight * mate[at].astype(F32)).astype(BF16)

    at_row = lax.broadcasted_iota(jnp.int32, (half, half), 0)
    at_col = lax.broadcasted_iota(jnp.int32, (half, half), 1)

    def lower(x):
        return jnp.where(at_row >= at_col, x, 0.0).astype(BF16)

    def upper(x):
        return jnp.where(at_row <= at_col, x, 0.0).astype(BF16)

    depth = idx // 2
    length = n_seq // 2

    def forward_local(h):
        sl = head_cols(h)
        q0, q1 = q[:half, sl], q[half:, sl]
        k0, k1 = k[:half, sl], k[half:, sl]
        v0, v1 = v[:half, sl], v[half:, sl]
        acc_a[:half, sl] = dot_nn(lower(dot_nt(q0, k0)), v0)
        acc_a[half:, sl] = dot_nn(dot_nt(q1, k0).astype(BF16), v0) + dot_nn(
            lower(dot_nt(q1, k1)), v1
        )
        scores[h, 0] = upper(dot_nt(k0, q0))
        scores[h, 1] = dot_nt(k0, q1).astype(BF16)
        scores[h, 2] = upper(dot_nt(k1, q1))

    def attend(h):
        sl = head_cols(h)
        attn[:, sl] = (acc_a[:, sl] + dot_nn(q[:, sl], pre[h])).astype(BF16)

    late = jnp.maximum(FORWARD_LAG * depth + GIVE_LAG, mine)

    def forward(i, carry):
        j = i - FORWARD_LAG * depth
        ready = (j >= 0) & (j < mine)

        @pl.when(ready)
        def _():
            pass_on(
                j, st, st_p, st_c, st_o, st_r, pre,
                (m_ss, m_rs, c_ss, c_rs, r_ss, r_rs),
                has_below, has_above, idx + 2, side,
            )

        @pl.when(i < heads)
        def _():
            forward_local(lax.rem(own_head + i, heads))

        @pl.when(ready)
        def _():
            attend(own_head + j)

        m = i - late

        @pl.when((m >= 0) & (m < mine))
        def _():
            head_copy(st_r, pre, r_ss, r_rs, mate_head, m, partner).wait_recv()
            attend(mate_head + m)

        return carry

    lax.fori_loop(0, max(FORWARD_LAG * (length - 1) + GIVE_LAG + mine, heads), forward, 0)

    br = 128

    def sums(c, carry):
        for p in range(len(peers)):
            w_arrival(p, c).wait_recv()

        def step(i, inner):
            rs = pl.ds(pl.multiple_of(i * br, br), br)
            s0 = jnp.zeros((br, hd), F32)
            s1 = jnp.zeros((br, hd), F32)
            for u in range(chunk // hd):
                at = pl.ds(pl.multiple_of(c * chunk + u * hd, hd), hd)
                a = attn[rs, at].astype(F32)
                w = wbuf[rs, at].astype(F32)
                s0 = s0 + a * a
                s1 = s1 + a * w
            squares[rs, :] += s0
            crossed[rs, :] += s1
            return inner

        lax.fori_loop(0, tok // br, step, 0)
        return carry

    squares[...] = jnp.zeros_like(squares)
    crossed[...] = jnp.zeros_like(crossed)
    lax.fori_loop(0, CHUNKS, sums, 0)
    n_row = tok // hd
    s0 = jnp.sum(jnp.transpose(squares[...]), axis=0, keepdims=True)
    s1 = jnp.sum(jnp.transpose(crossed[...]), axis=0, keepdims=True)
    for r in range(n_row):
        stat_s[r:r + 1, :] = s0[:, r * hd:(r + 1) * hd]
        stat_s[n_row + r:n_row + r + 1, :] = s1[:, r * hd:(r + 1) * hd]
    for p in range(len(peers)):
        s_copy(p).start()
    for c in range(CHUNKS):
        for p in range(len(peers)):
            a_copy(p, c).start()
    total = stat_s[...]
    for p in range(len(peers)):
        s_copy(p).wait_recv()
    for p in range(len(peers)):
        total = total + stat_r[p]
    inv = lax.rsqrt(total[:n_row] / width + EPS)
    c_all = inv * inv * (total[n_row:2 * n_row] / width)
    for r in range(n_row):
        inv_b[r * hd:(r + 1) * hd, :] = jnp.transpose(
            jnp.broadcast_to(inv[r:r + 1], (hd, hd))
        )
        c_b[r * hd:(r + 1) * hd, :] = jnp.transpose(
            jnp.broadcast_to(c_all[r:r + 1], (hd, hd))
        )

    def grads(base, group, send):
        def step(i, carry):
            first = base + group * i
            for t in range(group):
                sl = head_cols(first + t)
                a = attn[:, sl].astype(F32)
                grad = (inv_b[...] * (wbuf[:, sl].astype(F32) - a * c_b[...])).astype(BF16)
                d_o[:, sl] = grad
                gst[first + t] = dot_tn(q[:, sl], grad).astype(BF16)
            if send:
                for t in range(group):
                    head_copy(gst, gst_p, gm_ss, m_rs, base, i * group + t, partner).start()
            return carry

        lax.fori_loop(0, mine // group, step, 0)

    grads(mate_head, 2, True)
    grads(own_head, GROUP, False)

    def grad_scores(h, low, up):
        sl = head_cols(h)
        v0, v1 = v[:half, sl], v[half:, sl]
        d0, d1 = d_o[:half, sl], d_o[half:, sl]
        low[0] = lower(dot_nt(d0, v0))
        low[1] = dot_nt(d1, v0).astype(BF16)
        low[2] = lower(dot_nt(d1, v1))
        up[0] = upper(dot_nt(v0, d0))
        up[1] = dot_nt(v0, d1).astype(BF16)
        up[2] = upper(dot_nt(v1, d1))

    def grad_products(h, low, up):
        sl = head_cols(h)
        q0, q1 = q[:half, sl], q[half:, sl]
        k0, k1 = k[:half, sl], k[half:, sl]
        d0, d1 = d_o[:half, sl], d_o[half:, sl]
        before = pre[h]
        gqv[:half, sl] = (dot_nn(low[0], k0) + dot_nt(d0, before)).astype(BF16)
        gqv[half:, sl] = (
            dot_nn(low[1], k0) + dot_nn(low[2], k1) + dot_nt(d1, before)
        ).astype(BF16)
        acc_a[:half, sl] = dot_nn(up[0], q0) + dot_nn(up[1], q1)
        acc_a[half:, sl] = dot_nn(up[2], q1)
        acc_b[:half, sl] = dot_nn(scores[h, 0], d0) + dot_nn(scores[h, 1], d1)
        acc_b[half:, sl] = dot_nn(scores[h, 2], d1)

    back_lag = BACKWARD_LAG * (length - 1 - depth)
    slots = ((low_a, up_a), (low_b, up_b))

    def backward(i, carry):
        for t in range(2):
            h = 2 * i + t

            j = h - back_lag

            @pl.when((j >= 0) & (j < mine))
            def _():
                pass_on(
                    j, gst, gst_p, gst_c, gst_o, gst_r, suf,
                    (gm_ss, m_rs, gc_ss, c_rs, gr_ss, r_rs),
                    has_above, has_below, idx - 2, 1 - side,
                )

            @pl.when(h < heads)
            def _():
                grad_products(h, *slots[t])
                grad_scores(jnp.minimum(h + 1, heads - 1), *slots[1 - t])

        return carry

    steps = max(heads, BACKWARD_LAG * (length - 1) + mine)
    grad_scores(0, *slots[0])
    lax.fori_loop(0, (steps + 1) // 2, backward, 0)

    def finish(shard, c, local):
        scale = inv_b[row_block(me), :]
        for u in range(chunk // hd):
            at = pl.ds(pl.multiple_of(shard * cols + c * chunk + u * hd, hd), hd)
            if local:
                here = pl.ds(pl.multiple_of(c * chunk + u * hd, hd), hd)
                a = attn[row_block(me), here]
            else:
                a = arows[:, at]
            ggv[:, at] = (g2[:, at] * (a.astype(F32) * scale)).astype(BF16)

    def finish_local(c, carry):
        finish(me, c, True)
        return carry

    lax.fori_loop(0, CHUNKS, finish_local, 0)

    def finish_beside(c, carry):
        a_arrival(beside, c).wait_recv()
        finish(from_peer(beside), c, False)
        return carry

    lax.fori_loop(0, CHUNKS, finish_beside, 0)

    def finish_crossing(c, carry):
        for p in crossing:
            a_arrival(p, c).wait_recv()
            finish(from_peer(p), c, False)
        return carry

    lax.fori_loop(0, CHUNKS, finish_crossing, 0)

    for p in range(len(peers)):
        s_copy(p).wait_send()
    sent = len(peers)
    pltpu.make_async_remote_copy(
        src_ref=wsend.at[:, :sent * cols], dst_ref=arows.at[:, :sent * cols],
        send_sem=w_ss, recv_sem=w_rs.at[0],
        device_id={"head": to_peer(0)}, device_id_type=MESH,
    ).wait_send()
    pltpu.make_async_remote_copy(
        src_ref=attn.at[:sent * rows], dst_ref=wbuf.at[:sent * rows],
        send_sem=a_ss, recv_sem=a_rs.at[0],
        device_id={"head": to_peer(0)}, device_id_type=MESH,
    ).wait_send()
    heads_sent(st, st_p, m_ss, m_rs, mate_head, partner)
    heads_sent(st_r, pre, r_ss, r_rs, own_head, partner)
    heads_sent(gst, gst_p, gm_ss, m_rs, mate_head, partner)

    @pl.when(has_above)
    def _():
        heads_sent(st_o, st_c, c_ss, c_rs, own_head, idx + 2)

    @pl.when(has_below)
    def _():
        heads_sent(gst_o, gst_c, gc_ss, c_rs, own_head, idx - 2)

    def given(j, carry):
        head_copy(gst_r, suf, gr_ss, r_rs, mate_head, j, partner).wait_recv()
        return carry

    lax.fori_loop(0, mine, given, 0)
    heads_sent(gst_r, suf, gr_ss, r_rs, own_head, partner)


def store(gq, gg, acc_a, acc_b, suf, k, v, gq_h, gk_h, gv_h, gg_h, gk, gv, sem, k_sem, v_sem):
    hd = HEAD_DIM
    tok, cols = gq.shape
    span = GROUP * hd
    ready = [
        pltpu.make_async_copy(src, dst, sem.at[i])
        for i, (src, dst) in enumerate(((gq, gq_h), (gg, gg_h)))
    ]
    for copy in ready:
        copy.start()

    def copies(i):
        at = pl.ds(pl.multiple_of(i * span, span), span)
        return (
            pltpu.make_async_copy(gk.at[:, at], gk_h.at[:, at], k_sem.at[i]),
            pltpu.make_async_copy(gv.at[:, at], gv_h.at[:, at], v_sem.at[i]),
        )

    def add_later(i, carry):
        for t in range(GROUP):
            h = GROUP * i + t
            sl = pl.ds(pl.multiple_of(h * hd, hd), hd)
            after = suf[h]
            gk[:, sl] = (acc_a[:, sl] + dot_nt(v[:, sl], after)).astype(BF16)
            gv[:, sl] = (acc_b[:, sl] + dot_nn(k[:, sl], after)).astype(BF16)
        for copy in copies(i):
            copy.start()
        return carry

    groups = cols // span
    lax.fori_loop(0, groups, add_later, 0)
    for copy in ready:
        copy.wait()
    for i in range(groups):
        for copy in copies(i):
            copy.wait()


def on_device(n_seq, n_head, query, key_in, value, gate, gain, grad_out):
    tok, cols = query.shape
    rows, width = gate.shape
    heads = cols // HEAD_DIM
    groups = heads // GROUP
    wide = pltpu.VMEM((tok, cols), BF16)
    thin = pltpu.VMEM((rows, width), BF16)
    state = pltpu.VMEM((heads, HEAD_DIM, HEAD_DIM), BF16)
    token = pltpu.VMEM((tok, HEAD_DIM), F32)
    blocks = pltpu.VMEM((3, tok // 2, tok // 2), BF16)
    sum_of = pltpu.VMEM((tok, cols), F32)
    tile = (2 * tok // HEAD_DIM, HEAD_DIM)
    by_part = pltpu.SemaphoreType.DMA(((n_head - 1) * CHUNKS,))
    one = pltpu.SemaphoreType.DMA(())
    by_peer = pltpu.SemaphoreType.DMA((n_head - 1,))
    by_head = pltpu.SemaphoreType.DMA((heads // 2,))
    anywhere = pl.BlockSpec(memory_space=pl.ANY)
    on_chip = pl.BlockSpec(memory_space=pltpu.VMEM)
    results = pl.pallas_call(
        functools.partial(body, n_seq, n_head),
        out_shape=[wide, thin, sum_of, sum_of, state, wide, wide],
        in_specs=[anywhere] * 6,
        out_specs=[on_chip] * 7,
        scratch_shapes=[
            wide, thin, pltpu.VMEM((1, width), F32), thin,
            thin, wide, pltpu.VMEM((rows, width), F32), wide, wide, thin,
            state, state, state, state, state, state,
            state, state, state, state, state,
            pltpu.VMEM((heads, 3, tok // 2, tok // 2), BF16),
            blocks, blocks, blocks, blocks,
            token, token, pltpu.VMEM(tile, F32), pltpu.VMEM((n_head - 1, *tile), F32), token, token,
            pltpu.SemaphoreType.DMA((4,)), pltpu.SemaphoreType.DMA((2 * n_head,)),
            pltpu.SemaphoreType.DMA((2 * CHUNKS,)),
            one, by_part, one, by_part, by_peer, by_peer,
            one, by_head, one, by_head, one, by_head,
            one, one, one,
        ],
        compiler_params=pltpu.CompilerParams(
            collective_id=0, has_side_effects=True, vmem_limit_bytes=44 * 2**20
        ),
        name="linear_attention_backward",
    )(query, key_in, value, gate, gain.reshape(1, width), grad_out)
    wide_out = jax.ShapeDtypeStruct((tok, cols), BF16)
    return pl.pallas_call(
        store,
        out_shape=[wide_out, wide_out, wide_out, jax.ShapeDtypeStruct((rows, width), BF16)],
        in_specs=[on_chip] * 7,
        out_specs=[anywhere] * 4,
        scratch_shapes=[
            wide, wide, pltpu.SemaphoreType.DMA((2,)),
            pltpu.SemaphoreType.DMA((groups,)), pltpu.SemaphoreType.DMA((groups,)),
        ],
        compiler_params=pltpu.CompilerParams(vmem_limit_bytes=6 * 2**20),
        name="store_gradients",
    )(*[pltpu.with_memory_space_constraint(x, pltpu.VMEM) for x in results])


def solution(mesh):
    in_specs = (
        P("seq", "head"),
        P("seq", "head"),
        P("seq", "head"),
        P(("seq", "head"), None),
        P(),
        P(("seq", "head"), None),
    )
    out_specs = (P("seq", "head"), P("seq", "head"), P("seq", "head"), P(("seq", "head"), None))
    return jax.shard_map(
        functools.partial(on_device, mesh.shape["seq"], mesh.shape["head"]),
        mesh=mesh, in_specs=in_specs, out_specs=out_specs, check_vma=False,
    )
```

```python
import functools

import jax
import jax.numpy as jnp
from jax import lax
from jax.experimental import pallas as pl
from jax.experimental.pallas import tpu as pltpu
from jax.sharding import PartitionSpec as P

HEAD_DIM = 128
EPS = 1e-06
MESH = pl.DeviceIdType.MESH
F32 = jnp.float32
BF16 = jnp.bfloat16
CHUNKS = 4
GROUP = 4
FORWARD_LAG = 3
BACKWARD_LAG = 5
GIVE_LAG = 3
PARTS = 1


def dot_nn(a, b):
    return lax.dot_general(a, b, (((1,), (0,)), ((), ())), preferred_element_type=F32)


def dot_nt(a, b):
    return lax.dot_general(a, b, (((1,), (1,)), ((), ())), preferred_element_type=F32)


def dot_tn(a, b):
    return lax.dot_general(a, b, (((0,), (0,)), ((), ())), preferred_element_type=F32)


def body(
    n_seq, n_head,
    q_h, k_h, v_h, gate_h, gain_h, go_h,
    gqv, ggv, acc_a, acc_b, suf, k, v,
    q, gate, gain, go,
    wsend, wbuf, g2, attn, d_o, arows,
    st, st_p, st_c, st_o, st_r, pre,
    gst, gst_p, gst_c, gst_o, gst_r,
    scores, low_a, up_a, low_b, up_b, squares, crossed, stat_s, stat_r, inv_b, c_b,
    in_sem, part_sem, first_sem,
    w_ss, w_rs, a_ss, a_rs, s_ss, s_rs,
    m_ss, m_rs, c_ss, c_rs, r_ss, r_rs,
    gm_ss, gc_ss, gr_ss,
):
    hd = HEAD_DIM
    tok, cols = q.shape
    rows, width = gate.shape
    heads = cols // hd
    half = tok // 2
    mine = heads // 2
    chunk = cols // CHUNKS
    piece = hd // PARTS
    idx = lax.axis_index("seq")
    me = lax.axis_index("head")
    side = lax.rem(idx, 2)
    partner = idx + 1 - 2 * side
    has_below = idx >= 2
    has_above = idx + 2 < n_seq
    n_x = n_head // 2
    at_x = me // 2
    core = lax.rem(me, 2)
    peers = [(dx, dc) for dx in range(1, n_x) for dc in range(2)] + [(0, 1)]
    own_head = side * mine
    mate_head = (1 - side) * mine

    def to_peer(p):
        dx, dc = peers[p]
        return lax.rem(at_x + dx, n_x) * 2 + lax.rem(core + dc, 2)

    def from_peer(p):
        dx, dc = peers[p]
        return lax.rem(at_x + n_x - dx, n_x) * 2 + lax.rem(core + dc, 2)

    def row_block(shard):
        return pl.ds(pl.multiple_of(shard * rows, rows), rows)

    def col_block(shard):
        return pl.ds(pl.multiple_of(shard * cols, cols), cols)

    def col_chunk(shard, c):
        return pl.ds(pl.multiple_of(shard * cols + c * chunk, chunk), chunk)

    def head_cols(h):
        return pl.ds(pl.multiple_of(h * hd, hd), hd)

    whole_loads = [
        pltpu.make_async_copy(src, dst, in_sem.at[i])
        for i, (src, dst) in enumerate(((gain_h, gain), (k_h, k), (v_h, v), (q_h, q)))
    ]

    def part_load(i, shard):
        at = col_block(shard)
        return [
            pltpu.make_async_copy(gate_h.at[:, at], gate.at[:, at], part_sem.at[i]),
            pltpu.make_async_copy(go_h.at[:, at], go.at[:, at], part_sem.at[i]),
        ]

    shards = [to_peer(p) for p in range(len(peers))] + [me]

    def first_load(c):
        at = col_chunk(shards[0], c)
        return [
            pltpu.make_async_copy(gate_h.at[:, at], gate.at[:, at], first_sem.at[c]),
            pltpu.make_async_copy(go_h.at[:, at], go.at[:, at], first_sem.at[c]),
        ]

    whole_loads[0].start()
    for c in range(CHUNKS):
        for load in first_load(c):
            load.start()
    whole_loads[1].start()
    whole_loads[2].start()
    for i in range(1, len(shards)):
        for load in part_load(i, shards[i]):
            load.start()
    whole_loads[3].start()

    barrier = pltpu.get_barrier_semaphore()
    for p in range(len(peers)):
        pl.semaphore_signal(barrier, inc=1, device_id={"head": to_peer(p)}, device_id_type=MESH)
    pl.semaphore_signal(barrier, inc=1, device_id={"seq": partner}, device_id_type=MESH)

    @pl.when(has_below)
    def _():
        pl.semaphore_signal(barrier, inc=1, device_id={"seq": idx - 2}, device_id_type=MESH)

    @pl.when(has_above)
    def _():
        pl.semaphore_signal(barrier, inc=1, device_id={"seq": idx + 2}, device_id_type=MESH)

    bc = min(256, chunk)

    def weigh(shard, first, span, local):
        def step(i, carry):
            c = pl.multiple_of(first + i * bc, bc)
            at = pl.ds(pl.multiple_of(shard * cols + c, bc), bc)
            g = gate[:, at].astype(F32)
            scaled = go[:, at].astype(F32) * gain[:, at]
            sig = jax.nn.sigmoid(g)
            part = scaled * sig
            g2[:, at] = part * (1.0 + g * (1.0 - sig))
            weighted = (part * g).astype(BF16)
            if local:
                wbuf[row_block(me), pl.ds(c, bc)] = weighted
            else:
                wsend[:, at] = weighted
            return carry

        lax.fori_loop(0, span // bc, step, 0)

    def w_copy(p, c):
        to = to_peer(p)
        return pltpu.make_async_remote_copy(
            src_ref=wsend.at[:, col_chunk(to, c)],
            dst_ref=wbuf.at[row_block(me), col_chunk(0, c)],
            send_sem=w_ss, recv_sem=w_rs.at[c],
            device_id={"head": to}, device_id_type=MESH,
        )

    def w_arrivals(c):
        sent = len(peers) * rows
        pltpu.make_async_remote_copy(
            src_ref=attn.at[:sent, col_chunk(0, c)], dst_ref=wbuf.at[:sent, col_chunk(0, c)],
            send_sem=w_ss, recv_sem=w_rs.at[c],
            device_id={"head": to_peer(0)}, device_id_type=MESH,
        ).wait_recv()

    def a_copy(p, c):
        to = to_peer(p)
        return pltpu.make_async_remote_copy(
            src_ref=attn.at[row_block(to), col_chunk(0, c)],
            dst_ref=arows.at[:, col_chunk(me, c)],
            send_sem=a_ss, recv_sem=a_rs.at[c],
            device_id={"head": to}, device_id_type=MESH,
        )

    def a_arrivals(c):
        sent = len(peers) * rows
        pltpu.make_async_remote_copy(
            src_ref=attn.at[:sent, col_chunk(0, c)], dst_ref=wbuf.at[:sent, col_chunk(0, c)],
            send_sem=a_ss, recv_sem=a_rs.at[c],
            device_id={"head": to_peer(0)}, device_id_type=MESH,
        ).wait_recv()

    def s_copy(p):
        return pltpu.make_async_remote_copy(
            src_ref=stat_s, dst_ref=stat_r.at[p],
            send_sem=s_ss, recv_sem=s_rs,
            device_id={"head": to_peer(p)}, device_id_type=MESH,
        )

    def stats_moved():
        return pltpu.make_async_remote_copy(
            src_ref=stat_r, dst_ref=stat_r,
            send_sem=s_ss, recv_sem=s_rs,
            device_id={"head": to_peer(0)}, device_id_type=MESH,
        )

    def head_copy(src, dst, ss, rs, base, j, u, target):
        at = pl.ds(u * piece, piece)
        return pltpu.make_async_remote_copy(
            src_ref=src.at[base + j, at], dst_ref=dst.at[base + j, at],
            send_sem=ss, recv_sem=rs.at[PARTS * j + u],
            device_id={"seq": target}, device_id_type=MESH,
        )

    def heads_sent(src, dst, ss, rs, base, target):
        at = pl.ds(base, mine)
        pltpu.make_async_remote_copy(
            src_ref=src.at[at], dst_ref=dst.at[at],
            send_sem=ss, recv_sem=rs.at[0],
            device_id={"seq": target}, device_id_type=MESH,
        ).wait_send()

    def weigh_and_send(p):
        weigh(to_peer(p), 0, cols, False)
        for c in range(CHUNKS):
            w_copy(p, c).start()

    def wait_part(i):
        pltpu.make_async_copy(
            gate_h.at[:, :2 * cols], gate.at[:, :2 * cols], part_sem.at[i]
        ).wait()

    whole_loads[0].wait()
    for c in range(CHUNKS):
        pltpu.make_async_copy(
            gate_h.at[:, :2 * chunk], gate.at[:, :2 * chunk], first_sem.at[c]
        ).wait()
        weigh(shards[0], c * chunk, chunk, False)
        if c == 0:
            below, above = has_below.astype(jnp.int32), has_above.astype(jnp.int32)
            pl.semaphore_wait(barrier, n_head + below + above)
        w_copy(0, c).start()
    whole_loads[1].wait()
    whole_loads[2].wait()

    def states(base, send):
        def step(i, carry):
            first = base + GROUP * i
            for t in range(GROUP):
                sl = head_cols(first + t)
                st[first + t] = dot_tn(k[:, sl], v[:, sl]).astype(BF16)
            if send:
                for t in range(GROUP):
                    for u in range(PARTS):
                        head_copy(st, st_p, m_ss, m_rs, base, i * GROUP + t, u, partner).start()
            return carry

        lax.fori_loop(0, mine // GROUP, step, 0)

    states(mate_head, True)
    for p in range(1, len(peers)):
        wait_part(p)
        weigh_and_send(p)
    states(own_head, False)
    wait_part(len(peers))
    weigh(me, 0, cols, True)
    whole_loads[3].wait()

    def pass_on(j, own, mate, chain, out, given, kept, sems, source_ok, target_ok, target, wants):
        mate_ss, mate_rs, chain_ss, chain_rs, give_ss, give_rs = sems
        weight = wants.astype(F32)
        for u in range(PARTS):
            at = (own_head + j, slice(u * piece, (u + 1) * piece))
            head_copy(own, mate, mate_ss, mate_rs, own_head, j, u, partner).wait_recv()

            @pl.when(source_ok)
            def _():
                head_copy(out, chain, chain_ss, chain_rs, own_head, j, u, target).wait_recv()

            @pl.when(jnp.logical_not(source_ok))
            def _():
                chain[at] = jnp.zeros((piece, hd), BF16)

            @pl.when(target_ok)
            def _():
                out[at] = (
                    chain[at].astype(F32) + mate[at].astype(F32) + own[at].astype(F32)
                ).astype(BF16)
                head_copy(out, chain, chain_ss, chain_rs, own_head, j, u, target).start()

            before = chain[at].astype(F32)
            given[at] = (before + (1.0 - weight) * own[at].astype(F32)).astype(BF16)
            head_copy(given, kept, give_ss, give_rs, own_head, j, u, partner).start()
            kept[at] = (before + weight * mate[at].astype(F32)).astype(BF16)

    at_row = lax.broadcasted_iota(jnp.int32, (half, half), 0)
    at_col = lax.broadcasted_iota(jnp.int32, (half, half), 1)

    def lower(x):
        return jnp.where(at_row >= at_col, x, 0.0).astype(BF16)

    def upper(x):
        return jnp.where(at_row <= at_col, x, 0.0).astype(BF16)

    depth = idx // 2
    length = n_seq // 2

    def forward_local(h):
        sl = head_cols(h)
        q0, q1 = q[:half, sl], q[half:, sl]
        k0, k1 = k[:half, sl], k[half:, sl]
        v0, v1 = v[:half, sl], v[half:, sl]
        acc_a[:half, sl] = dot_nn(lower(dot_nt(q0, k0)), v0)
        acc_a[half:, sl] = dot_nn(dot_nt(q1, k0).astype(BF16), v0) + dot_nn(
            lower(dot_nt(q1, k1)), v1
        )
        scores[h, 0] = upper(dot_nt(k0, q0))
        scores[h, 1] = dot_nt(k0, q1).astype(BF16)
        scores[h, 2] = upper(dot_nt(k1, q1))

    def attend(h):
        sl = head_cols(h)
        attn[:, sl] = (acc_a[:, sl] + dot_nn(q[:, sl], pre[h])).astype(BF16)

    late = jnp.maximum(FORWARD_LAG * depth + GIVE_LAG, mine)

    def forward(i, carry):
        j = i - FORWARD_LAG * depth
        ready = (j >= 0) & (j < mine)

        @pl.when(ready)
        def _():
            pass_on(
                j, st, st_p, st_c, st_o, st_r, pre,
                (m_ss, m_rs, c_ss, c_rs, r_ss, r_rs),
                has_below, has_above, idx + 2, side,
            )

        @pl.when(i < heads)
        def _():
            forward_local(lax.rem(own_head + i, heads))

        @pl.when(ready)
        def _():
            attend(own_head + j)

        m = i - late

        @pl.when((m >= 0) & (m < mine))
        def _():
            for u in range(PARTS):
                head_copy(st_r, pre, r_ss, r_rs, mate_head, m, u, partner).wait_recv()
            attend(mate_head + m)

        return carry

    lax.fori_loop(0, max(FORWARD_LAG * (length - 1) + GIVE_LAG + mine, heads), forward, 0)

    br = 128

    def sums(c, carry):
        w_arrivals(c)

        def step(i, inner):
            rs = pl.ds(pl.multiple_of(i * br, br), br)
            s0 = jnp.zeros((br, hd), F32)
            s1 = jnp.zeros((br, hd), F32)
            for u in range(chunk // hd):
                at = pl.ds(pl.multiple_of(c * chunk + u * hd, hd), hd)
                a = attn[rs, at].astype(F32)
                w = wbuf[rs, at].astype(F32)
                s0 = s0 + a * a
                s1 = s1 + a * w
            squares[rs, :] += s0
            crossed[rs, :] += s1
            return inner

        lax.fori_loop(0, tok // br, step, 0)
        return carry

    squares[...] = jnp.zeros_like(squares)
    crossed[...] = jnp.zeros_like(crossed)
    lax.fori_loop(0, CHUNKS, sums, 0)
    n_row = tok // hd
    s0 = jnp.sum(jnp.transpose(squares[...]), axis=0, keepdims=True)
    s1 = jnp.sum(jnp.transpose(crossed[...]), axis=0, keepdims=True)
    for r in range(n_row):
        stat_s[r:r + 1, :] = s0[:, r * hd:(r + 1) * hd]
        stat_s[n_row + r:n_row + r + 1, :] = s1[:, r * hd:(r + 1) * hd]
    for p in range(len(peers)):
        s_copy(p).start()
    for c in range(CHUNKS):
        for p in range(len(peers)):
            a_copy(p, c).start()
    total = stat_s[...]
    stats_moved().wait_recv()
    for p in range(len(peers)):
        total = total + stat_r[p]
    inv = lax.rsqrt(total[:n_row] / width + EPS)
    c_all = inv * inv * (total[n_row:2 * n_row] / width)
    for r in range(n_row):
        inv_b[r * hd:(r + 1) * hd, :] = jnp.transpose(
            jnp.broadcast_to(inv[r:r + 1], (hd, hd))
        )
        c_b[r * hd:(r + 1) * hd, :] = jnp.transpose(
            jnp.broadcast_to(c_all[r:r + 1], (hd, hd))
        )

    def grads(base, group, send):
        def step(i, carry):
            first = base + group * i
            for t in range(group):
                sl = head_cols(first + t)
                a = attn[:, sl].astype(F32)
                grad = (inv_b[...] * (wbuf[:, sl].astype(F32) - a * c_b[...])).astype(BF16)
                d_o[:, sl] = grad
                gst[first + t] = dot_tn(q[:, sl], grad).astype(BF16)
            if send:
                for t in range(group):
                    for u in range(PARTS):
                        head_copy(gst, gst_p, gm_ss, m_rs, base, i * group + t, u, partner).start()
            return carry

        lax.fori_loop(0, mine // group, step, 0)

    grads(mate_head, 2, True)
    grads(own_head, GROUP, False)

    def grad_scores(h, low, up):
        sl = head_cols(h)
        v0, v1 = v[:half, sl], v[half:, sl]
        d0, d1 = d_o[:half, sl], d_o[half:, sl]
        low[0] = lower(dot_nt(d0, v0))
        low[1] = dot_nt(d1, v0).astype(BF16)
        low[2] = lower(dot_nt(d1, v1))
        up[0] = upper(dot_nt(v0, d0))
        up[1] = dot_nt(v0, d1).astype(BF16)
        up[2] = upper(dot_nt(v1, d1))

    def grad_products(h, low, up):
        sl = head_cols(h)
        q0, q1 = q[:half, sl], q[half:, sl]
        k0, k1 = k[:half, sl], k[half:, sl]
        d0, d1 = d_o[:half, sl], d_o[half:, sl]
        before = pre[h]
        gqv[:half, sl] = (dot_nn(low[0], k0) + dot_nt(d0, before)).astype(BF16)
        gqv[half:, sl] = (
            dot_nn(low[1], k0) + dot_nn(low[2], k1) + dot_nt(d1, before)
        ).astype(BF16)
        acc_a[:half, sl] = dot_nn(up[0], q0) + dot_nn(up[1], q1)
        acc_a[half:, sl] = dot_nn(up[2], q1)
        acc_b[:half, sl] = dot_nn(scores[h, 0], d0) + dot_nn(scores[h, 1], d1)
        acc_b[half:, sl] = dot_nn(scores[h, 2], d1)

    from_end = length - 1 - depth
    back_lag = BACKWARD_LAG * from_end + jnp.minimum(from_end, 1)
    slots = ((low_a, up_a), (low_b, up_b))

    def backward(i, carry):
        for t in range(2):
            h = 2 * i + t

            j = h - back_lag

            @pl.when((j >= 0) & (j < mine))
            def _():
                pass_on(
                    j, gst, gst_p, gst_c, gst_o, gst_r, suf,
                    (gm_ss, m_rs, gc_ss, c_rs, gr_ss, r_rs),
                    has_above, has_below, idx - 2, 1 - side,
                )

            @pl.when(h < heads)
            def _():
                grad_products(h, *slots[t])
                grad_scores(jnp.minimum(h + 1, heads - 1), *slots[1 - t])

        return carry

    steps = max(heads, BACKWARD_LAG * (length - 1) + 1 + mine)
    grad_scores(0, *slots[0])
    lax.fori_loop(0, (steps + 1) // 2, backward, 0)

    def finish(shard, c, local):
        scale = inv_b[row_block(me), :]
        for u in range(chunk // hd):
            at = pl.ds(pl.multiple_of(shard * cols + c * chunk + u * hd, hd), hd)
            if local:
                here = pl.ds(pl.multiple_of(c * chunk + u * hd, hd), hd)
                a = attn[row_block(me), here]
            else:
                a = arows[:, at]
            ggv[:, at] = (g2[:, at] * (a.astype(F32) * scale)).astype(BF16)

    def finish_local(c, carry):
        finish(me, c, True)
        return carry

    lax.fori_loop(0, CHUNKS, finish_local, 0)

    def finish_sent(c, carry):
        a_arrivals(c)
        for p in range(len(peers)):
            finish(from_peer(p), c, False)
        return carry

    lax.fori_loop(0, CHUNKS, finish_sent, 0)

    stats_moved().wait_send()
    sent = len(peers)
    pltpu.make_async_remote_copy(
        src_ref=wsend.at[:, :sent * cols], dst_ref=arows.at[:, :sent * cols],
        send_sem=w_ss, recv_sem=w_rs.at[0],
        device_id={"head": to_peer(0)}, device_id_type=MESH,
    ).wait_send()
    pltpu.make_async_remote_copy(
        src_ref=attn.at[:sent * rows], dst_ref=wbuf.at[:sent * rows],
        send_sem=a_ss, recv_sem=a_rs.at[0],
        device_id={"head": to_peer(0)}, device_id_type=MESH,
    ).wait_send()
    heads_sent(st, st_p, m_ss, m_rs, mate_head, partner)
    heads_sent(st_r, pre, r_ss, r_rs, own_head, partner)
    heads_sent(gst, gst_p, gm_ss, m_rs, mate_head, partner)

    @pl.when(has_above)
    def _():
        heads_sent(st_o, st_c, c_ss, c_rs, own_head, idx + 2)

    @pl.when(has_below)
    def _():
        heads_sent(gst_o, gst_c, gc_ss, c_rs, own_head, idx - 2)

    def given(j, carry):
        for u in range(PARTS):
            head_copy(gst_r, suf, gr_ss, r_rs, mate_head, j, u, partner).wait_recv()
        return carry

    lax.fori_loop(0, mine, given, 0)
    heads_sent(gst_r, suf, gr_ss, r_rs, own_head, partner)


def store(gq, gg, acc_a, acc_b, suf, k, v, gq_h, gk_h, gv_h, gg_h, gk, gv, sem, k_sem, v_sem):
    hd = HEAD_DIM
    tok, cols = gq.shape
    span = GROUP * hd
    ready = [
        pltpu.make_async_copy(src, dst, sem.at[i])
        for i, (src, dst) in enumerate(((gq, gq_h), (gg, gg_h)))
    ]
    for copy in ready:
        copy.start()

    def copies(i):
        at = pl.ds(pl.multiple_of(i * span, span), span)
        return (
            pltpu.make_async_copy(gk.at[:, at], gk_h.at[:, at], k_sem.at[i]),
            pltpu.make_async_copy(gv.at[:, at], gv_h.at[:, at], v_sem.at[i]),
        )

    def add_later(i, carry):
        for t in range(GROUP):
            h = GROUP * i + t
            sl = pl.ds(pl.multiple_of(h * hd, hd), hd)
            after = suf[h]
            gk[:, sl] = (acc_a[:, sl] + dot_nt(v[:, sl], after)).astype(BF16)
            gv[:, sl] = (acc_b[:, sl] + dot_nn(k[:, sl], after)).astype(BF16)
        for copy in copies(i):
            copy.start()
        return carry

    groups = cols // span
    lax.fori_loop(0, groups, add_later, 0)
    for copy in ready:
        copy.wait()
    for i in range(groups):
        for copy in copies(i):
            copy.wait()


def on_device(n_seq, n_head, query, key_in, value, gate, gain, grad_out):
    tok, cols = query.shape
    rows, width = gate.shape
    heads = cols // HEAD_DIM
    groups = heads // GROUP
    wide = pltpu.VMEM((tok, cols), BF16)
    thin = pltpu.VMEM((rows, width), BF16)
    state = pltpu.VMEM((heads, HEAD_DIM, HEAD_DIM), BF16)
    token = pltpu.VMEM((tok, HEAD_DIM), F32)
    blocks = pltpu.VMEM((3, tok // 2, tok // 2), BF16)
    sum_of = pltpu.VMEM((tok, cols), F32)
    tile = (2 * tok // HEAD_DIM, HEAD_DIM)
    by_chunk = pltpu.SemaphoreType.DMA((CHUNKS,))
    one = pltpu.SemaphoreType.DMA(())
    by_head = pltpu.SemaphoreType.DMA((heads // 2 * PARTS,))
    anywhere = pl.BlockSpec(memory_space=pl.ANY)
    on_chip = pl.BlockSpec(memory_space=pltpu.VMEM)
    results = pl.pallas_call(
        functools.partial(body, n_seq, n_head),
        out_shape=[wide, thin, sum_of, sum_of, state, wide, wide],
        in_specs=[anywhere] * 6,
        out_specs=[on_chip] * 7,
        scratch_shapes=[
            wide, thin, pltpu.VMEM((1, width), F32), thin,
            thin, wide, pltpu.VMEM((rows, width), F32), wide, wide, thin,
            state, state, state, state, state, state,
            state, state, state, state, state,
            pltpu.VMEM((heads, 3, tok // 2, tok // 2), BF16),
            blocks, blocks, blocks, blocks,
            token, token, pltpu.VMEM(tile, F32), pltpu.VMEM((n_head - 1, *tile), F32), token, token,
            pltpu.SemaphoreType.DMA((4,)), pltpu.SemaphoreType.DMA((n_head,)), by_chunk,
            one, by_chunk, one, by_chunk, one, one,
            one, by_head, one, by_head, one, by_head,
            one, one, one,
        ],
        compiler_params=pltpu.CompilerParams(
            collective_id=0, has_side_effects=True, vmem_limit_bytes=44 * 2**20
        ),
        name="linear_attention_backward",
    )(query, key_in, value, gate, gain.reshape(1, width), grad_out)
    wide_out = jax.ShapeDtypeStruct((tok, cols), BF16)
    return pl.pallas_call(
        store,
        out_shape=[wide_out, wide_out, wide_out, jax.ShapeDtypeStruct((rows, width), BF16)],
        in_specs=[on_chip] * 7,
        out_specs=[anywhere] * 4,
        scratch_shapes=[
            wide, wide, pltpu.SemaphoreType.DMA((2,)),
            pltpu.SemaphoreType.DMA((groups,)), pltpu.SemaphoreType.DMA((groups,)),
        ],
        compiler_params=pltpu.CompilerParams(vmem_limit_bytes=6 * 2**20),
        name="store_gradients",
    )(*[pltpu.with_memory_space_constraint(x, pltpu.VMEM) for x in results])


def solution(mesh):
    in_specs = (
        P("seq", "head"),
        P("seq", "head"),
        P("seq", "head"),
        P(("seq", "head"), None),
        P(),
        P(("seq", "head"), None),
    )
    out_specs = (P("seq", "head"), P("seq", "head"), P("seq", "head"), P(("seq", "head"), None))
    return jax.shard_map(
        functools.partial(on_device, mesh.shape["seq"], mesh.shape["head"]),
        mesh=mesh, in_specs=in_specs, out_specs=out_specs, check_vma=False,
    )
```
